32 devices in a mesh: row: 4 (over z), col: 8 (over y, x, core).
Axes of the slice: x: 2, y: 2, z: 4, core: 2. Of those that a mesh axis runs over, the one named last changes fastest.
Arguments:
- train_embed: bfloat16 [2048, 256], P(('row', 'col')), may hold values from -16 to 16
- valid_embed: bfloat16 [16384, 256], P(('row', 'col')), may hold values from -16 to 16
- train_labels: int32 [2048], P(('row', 'col')), may hold values from 0 to 99
- valid_labels: int32 [16384], P(('row', 'col')), may hold values from 0 to 99
- pair_level: int32 [100, 100], replicated, may hold values from 0 to 3
- level_cost: float32 [4], replicated, may hold values from 0.05 to 1
Outputs:
- calibrated: float32 [2048], P('row')
The draws below stay inside these ranges and needn't reach their ends.
All inputs are finite; a program needn't handle non-finite values.
Results may differ from the reference program's by a relative error of at most 0.0003.
Values may be sent and summed in bfloat16 or wider, within the bound.
A program may use at most 64 MiB of HBM per device.

```python
import math
import jax
import jax.numpy as jnp
import numpy as np
from jax import lax

EMBED = 256
CLASSES = 100
LEVELS = 4
ITERS = 4
TRAIN_PTS = 2048
VALID_PTS = 16384


def embed_pair(key):
    base = jax.random.fold_in(key, 7)
    train_draw = jax.random.normal(jax.random.fold_in(base, 1), (TRAIN_PTS, EMBED), jnp.float32)
    valid_draw = jax.random.normal(jax.random.fold_in(base, 2), (VALID_PTS, EMBED), jnp.float32)
    return (jnp.clip(train_draw, -16.0, 16.0), jnp.clip(valid_draw, -16.0, 16.0))


def draw_train_embed(key, part):
    return embed_pair(key)[0].astype(jnp.bfloat16)


def draw_valid_embed(key, part):
    return embed_pair(key)[1].astype(jnp.bfloat16)


def place_ends(entries, stream_key, smallest, largest):
    extent = entries.shape
    index_at = [jax.random.randint(jax.random.fold_in(stream_key, axis), (), 0, extent[axis]) for axis in range(len(extent))]
    entries = entries.at[tuple(index_at)].set(smallest)
    longest = extent.index(max(extent))
    index_at[longest] = (index_at[longest] + 1) % extent[longest]
    return entries.at[tuple(index_at)].set(largest)


def cumulative_ranks(amount, lean):
    portions = [(1 << 20) // math.isqrt(grade ** lean) + 1 for grade in range(1, amount + 1)]
    spread = 1 + sum(portions) // (1 << 30)
    return np.cumsum(np.array([max(1, weight // spread) for weight in portions]))


def ranked_ids(stream_key, extent, amount, lean):
    table = cumulative_ranks(amount, lean)
    lot = jax.random.randint(jax.random.fold_in(stream_key, 1), extent, 0, int(table[amount - 1]))
    rank = jnp.searchsorted(jnp.asarray(table, jnp.int32), lot, side="right")
    return jax.random.permutation(jax.random.fold_in(stream_key, 2), amount)[rank].astype(jnp.int32)


def setup_inputs(seed: int = 0) -> dict:
    arg_keys = jax.random.split(jax.random.key(seed), 7)
    return {
        "train_embed": draw_train_embed(jax.random.fold_in(arg_keys[6], 71), 0),
        "valid_embed": draw_valid_embed(jax.random.fold_in(arg_keys[6], 71), 0),
        "train_labels": place_ends(ranked_ids(arg_keys[2], (TRAIN_PTS,), CLASSES, 2), jax.random.fold_in(arg_keys[2], 3), 0, CLASSES - 1).astype(jnp.int32),
        "valid_labels": place_ends(ranked_ids(arg_keys[3], (VALID_PTS,), CLASSES, 2), jax.random.fold_in(arg_keys[3], 3), 0, CLASSES - 1).astype(jnp.int32),
        "pair_level": place_ends(jax.random.randint(arg_keys[4], (CLASSES, CLASSES), 0, LEVELS), jax.random.fold_in(arg_keys[4], 1), 0, LEVELS - 1).astype(jnp.int32),
        "level_cost": jnp.clip(jnp.exp(jax.random.uniform(arg_keys[5], (LEVELS,), jnp.float32, math.log(0.05), math.log(1.0))), 0.05, 1.0),
    }


entropy_scale = 0.05


def class_costs(pair_level, level_cost):
    selected = (pair_level[:, :, None] == jnp.arange(LEVELS, dtype=jnp.int32)[None, None, :]).astype(jnp.float32)
    return jnp.sum(selected * level_cost[None, None, :], axis=2)


def reference(train_embed, valid_embed, train_labels, valid_labels, pair_level, level_cost):
    class_table = class_costs(pair_level, level_cost)
    train_wide = train_embed.astype(jnp.float32)
    train_sq = jnp.sum(train_wide * train_wide, axis=1)
    row_labels = class_table[train_labels]
    block_cols = min(512, VALID_PTS)
    block_count = VALID_PTS // block_cols
    valid_blocks = valid_embed.reshape(block_count, block_cols, EMBED)
    label_blocks = valid_labels.reshape(block_count, block_cols)
    row_pot = jnp.zeros((TRAIN_PTS,), jnp.float32)
    col_pot = jnp.zeros((VALID_PTS,), jnp.float32)
    for iteration in range(ITERS):
        def visit(running, inputs, row_pot=row_pot):
            block_y, block_labels, block_pot = inputs
            block_wide = block_y.astype(jnp.float32)
            block_sq = jnp.sum(block_wide * block_wide, axis=1)
            products = jnp.dot(train_embed, block_y.T, preferred_element_type=jnp.float32)
            cost_tile = (train_sq[:, None] + block_sq[None, :] - 2.0 * products) / EMBED + row_labels[:, block_labels]
            row_side = (block_pot[None, :] - cost_tile) / entropy_scale
            col_side = (row_pot[:, None] - cost_tile) / entropy_scale
            return jnp.logaddexp(running, jax.nn.logsumexp(row_side, axis=1)), jax.nn.logsumexp(col_side, axis=0)

        start_lse = jnp.full((TRAIN_PTS,), -jnp.inf, jnp.float32)
        row_lse, col_lse = lax.scan(visit, start_lse, (valid_blocks, label_blocks, col_pot.reshape(block_count, block_cols)))
        col_lse = col_lse.reshape(VALID_PTS)
        row_new = entropy_scale * math.log(VALID_PTS) - entropy_scale * row_lse
        col_new = entropy_scale * math.log(TRAIN_PTS) - entropy_scale * col_lse
        row_pot = 0.5 * (row_pot + row_new)
        col_pot = 0.5 * (col_pot + col_new)
    potential_sum = jnp.sum(row_pot)
    return (row_pot * TRAIN_PTS - potential_sum) / (TRAIN_PTS - 1)
```

```python
import functools
import math

import jax
import jax.numpy as jnp
from jax import lax
from jax.experimental import pallas as pl
from jax.experimental.pallas import tpu as pltpu
from jax.sharding import PartitionSpec as P

ITERS = 4
entropy_scale = 0.05
SCALE = math.log2(math.e) / entropy_scale
LOG2E = math.log2(math.e)
NT = (((1,), (1,)), ((), ()))
LANES = 128


def log2(x):
    return jnp.log(x) * LOG2E


def pieces(x, count):
    out = []
    for _ in range(count):
        part = x.astype(jnp.bfloat16)
        out.append(part)
        x = x - part.astype(jnp.float32)
    return out


def dot(a, b, dims=(((1,), (0,)), ((), ()))):
    return lax.dot_general(a, b, dims, preferred_element_type=jnp.float32)


def kernel(nr, nc, n, level_ref, pair_ref, block_ref, valid_ref, vlab_ref, out_ref,
           buf, cost, y_ref, b_ref, a_ref, norm_ref, table_ref, pbuf, zbuf,
           local_sem, gsend1, gsend2, gsend3, grecv, psend, precv, zsend, zrecv):
    width = valid_ref.shape[1]
    nv = valid_ref.shape[0]
    nt = nr * nc * n
    nh = nc // 2
    kap = SCALE / width
    r = lax.axis_index("row")
    c = lax.axis_index("col")
    hi = c // 2
    lo = c % 2
    partner = hi * 2 + (1 - lo)
    me = r * nc + c

    def rc(src, dst, ss, rs, row, col):
        return pltpu.make_async_remote_copy(
            src_ref=src, dst_ref=dst, send_sem=ss, recv_sem=rs,
            device_id={"row": row, "col": col}, device_id_type=pl.DeviceIdType.MESH)

    def loop(lower, upper, body):
        if upper - lower <= 8:
            for i in range(lower, upper):
                body(i)
        else:
            lax.fori_loop(lower, upper, lambda i, _: (body(i), 0)[1], 0)

    barrier = pltpu.get_barrier_semaphore()
    loop(1, nr, lambda d: pl.semaphore_signal(
        barrier, inc=1, device_id={"row": (r + d) % nr, "col": c}, device_id_type=pl.DeviceIdType.MESH))
    loop(1, nc, lambda d: pl.semaphore_signal(
        barrier, inc=1, device_id={"row": r, "col": (c + d) % nc}, device_id_type=pl.DeviceIdType.MESH))
    own = pltpu.make_async_copy(block_ref, buf.at[me], local_sem)
    own.start()
    pl.semaphore_wait(barrier, nr + nc - 2)

    def to_row(d):
        return rc(block_ref, buf.at[me], gsend1.at[d], grecv.at[me], (r + d) % nr, c)

    def to_plane(src, b, dr, d):
        return rc(src, buf.at[b], gsend2.at[dr, d], grecv.at[b], r, ((hi + d) % nh) * 2 + lo)

    def to_partner(src, b, k):
        return rc(src, buf.at[b], gsend3.at[k], grecv.at[b], r, partner)

    def arrived(b):
        rc(buf.at[b], buf.at[b], local_sem, grecv.at[b], r, partner).wait_recv()

    loop(1, nr, lambda d: to_row(d).start())
    loop(1, nh, lambda d: to_plane(block_ref, me, 0, d).start())
    to_partner(block_ref, me, 0).start()

    valid = valid_ref[...]
    wide = valid.astype(jnp.float32)
    b_ref[...] = jnp.broadcast_to(-kap * jnp.sum(wide * wide, axis=1, keepdims=True), b_ref.shape)
    classes = pair_ref.shape[0]
    pair = pair_ref[...]
    table = jnp.zeros(pair.shape, jnp.float32)
    for level in range(level_ref.shape[0]):
        table = table + jnp.where(pair == level, level_ref[level], 0.0)
    table_ref[...] = jnp.zeros_like(table_ref)
    table_ref[0:classes, 0:classes] = table * (-0.5 * width)
    hot = (lax.broadcasted_iota(jnp.int32, (LANES, nv), 0) == vlab_ref[...]).astype(jnp.float32)
    hot = hot.T.astype(jnp.bfloat16)
    for k, part in enumerate(pieces(table_ref[...], 3)):
        y_ref[k] = dot(hot, part, NT).astype(jnp.bfloat16)

    def forward_row(d):
        b = ((r + nr - d) % nr) * nc + c
        arrived(b)
        loop(1, nh, lambda e: to_plane(buf.at[b], b, d, e).start())
        to_partner(buf.at[b], b, d * nh).start()

    loop(1, nr, forward_row)

    def forward_plane(d):
        def one(e):
            b = ((r + nr - d) % nr) * nc + ((hi + nh - e) % nh) * 2 + lo
            arrived(b)
            to_partner(buf.at[b], b, d * nh + e).start()
        loop(1, nh, one)

    loop(0, nr, forward_plane)
    loop(0, nr, lambda d: loop(0, nh, lambda e: arrived(
        ((r + nr - d) % nr) * nc + ((hi + nh - e) % nh) * 2 + (1 - lo))))
    own.wait()

    chunk = 256
    per = chunk // n
    ones = jnp.ones((8, width), jnp.bfloat16)

    def build(m, _):
        rows = buf[pl.ds(m * per, per), 0:n, :].reshape(chunk, width)
        lane = lax.broadcasted_iota(jnp.int32, (1, chunk), 1) // n
        labels = jnp.zeros((1, chunk), jnp.float32)
        for q in range(per):
            extra = buf[m * per + q, n:n + 16, :].astype(jnp.float32)
            labels = jnp.where(lane == q, extra[0:1, 0:chunk], labels)
        ids = lax.broadcasted_iota(jnp.int32, (LANES, chunk), 0)
        t_hot = (ids == labels.astype(jnp.int32)).astype(jnp.float32).astype(jnp.bfloat16)
        total = dot(valid_ref[...], rows, NT)
        for k in range(3):
            total = total + dot(y_ref[k], t_hot)
        at = pl.ds(pl.multiple_of(m * chunk, chunk), chunk)
        cost[:, at] = total * (2.0 * kap)
        wide = rows.astype(jnp.float32)
        high, low = pieces(wide * wide, 2)
        sq = dot(ones, high, NT) + dot(ones, low, NT)
        norm_ref[:, at] = sq[0:1] * kap
        return 0

    lax.fori_loop(0, nt // chunk, build, 0)
    a_ref[0] = -norm_ref[...]

    full_rows = nt
    full_cols = nv * nr * nc
    span = 512

    def row_side(e):
        for w in range(nt // span):
            at = slice(w * span, (w + 1) * span)

            def term(k):
                rows = pl.ds(pl.multiple_of(k * 8, 8), 8)
                pot = b_ref[rows, :]
                return cost[rows, at] + jnp.concatenate([pot] * (span // LANES), axis=1)

            high = lax.fori_loop(0, nv // 8, lambda k, h: jnp.maximum(h, term(k)),
                                 jnp.full((8, span), -jnp.inf, jnp.float32), unroll=8)
            high = jnp.max(high, axis=0, keepdims=True)
            wide_high = jnp.broadcast_to(high, (8, span))
            total = lax.fori_loop(0, nv // 8, lambda k, s: s + jnp.exp2(term(k) - wide_high),
                                  jnp.zeros((8, span), jnp.float32), unroll=8)
            total = jnp.sum(total, axis=0, keepdims=True)
            pbuf[e, c, :, at] = high + log2(total)

    def col_side(a):
        pot = jnp.broadcast_to(a, (8, nt))

        def one(k, _):
            rows = pl.ds(pl.multiple_of(k * 8, 8), 8)
            t = cost[rows, :] + pot
            high = jnp.max(t, axis=1, keepdims=True)
            total = jnp.sum(jnp.exp2(t - high), axis=1, keepdims=True)
            new = math.log2(full_rows) - (high + log2(total))
            b_ref[rows, :] = 0.5 * (b_ref[rows, :] + new)
            return 0

        lax.fori_loop(0, nv // 8, one, 0, unroll=4)

    def p_copy(e, d, to):
        src = c if to else (c + nc - d) % nc
        return rc(pbuf.at[e, src], pbuf.at[e, src], psend.at[e, d], precv.at[e, d], r, (c + d) % nc)

    def z_copy(e, d, to):
        src = r if to else (r + nr - d) % nr
        return rc(zbuf.at[e, src], zbuf.at[e, src], zsend.at[e, d], zrecv.at[e, d], (r + d) % nr, c)

    def joined(parts):
        high = jnp.max(parts, axis=0)
        return high + log2(jnp.sum(jnp.exp2(parts - high[None]), axis=0))

    def send_plane(e):
        loop(1, nc, lambda d: p_copy(e, d, True).start())

    def turn(e):
        loop(1, nc, lambda d: p_copy(e, d, False).wait_recv())
        zbuf[e, r] = joined(pbuf[e])
        loop(1, nr, lambda d: z_copy(e, d, True).start())

    def finish(e):
        loop(1, nr, lambda d: z_copy(e, d, False).wait_recv())
        a_ref[e + 1] = 0.5 * (a_ref[e] + (math.log2(full_cols) - joined(zbuf[e])))

    row_side(0)
    send_plane(0)
    col_side(a_ref[0])
    row_side(1)
    send_plane(1)
    for e in range(0, ITERS, 2):
        turn(e)
        turn(e + 1)
        finish(e)
        if e + 2 < ITERS:
            col_side(a_ref[e + 1])
            row_side(e + 2)
            send_plane(e + 2)
        finish(e + 1)
        if e + 3 < ITERS:
            col_side(a_ref[e + 2])
            row_side(e + 3)
            send_plane(e + 3)

    row_pot = (a_ref[ITERS] + norm_ref[...]) * (1.0 / SCALE)
    result = (row_pot * full_rows - jnp.sum(row_pot, axis=1, keepdims=True)) * (1.0 / (full_rows - 1))
    norm_ref[...] = result
    span_out = nt // nr
    out_ref[...] = norm_ref[:, pl.ds(pl.multiple_of(r * span_out, span_out), span_out)]

    loop(1, nr, lambda d: to_row(d).wait_send())
    loop(0, nr, lambda d: loop(1, nh, lambda e: to_plane(block_ref, me, d, e).wait_send()))
    loop(0, nr, lambda d: loop(0, nh, lambda e: to_partner(block_ref, me, d * nh + e).wait_send()))
    for e in range(ITERS):
        loop(1, nc, lambda d: p_copy(e, d, True).wait_send())
        loop(1, nr, lambda d: z_copy(e, d, True).wait_send())


def solution(mesh):
    nr, nc = mesh.shape["row"], mesh.shape["col"]

    def shards(train_embed, valid_embed, train_labels, valid_labels, pair_level, level_cost):
        n, width = train_embed.shape
        nv = valid_embed.shape[0]
        nt = nr * nc * n
        labels = jnp.tile(train_labels.astype(jnp.bfloat16), width // n)[None, :]
        block = jnp.concatenate([train_embed, jnp.broadcast_to(labels, (16, width))], axis=0)
        vmem = pl.BlockSpec(memory_space=pltpu.VMEM)
        dma = pltpu.SemaphoreType.DMA
        out = pl.pallas_call(
            functools.partial(kernel, nr, nc, n),
            out_shape=jax.ShapeDtypeStruct((1, nt // nr), jnp.float32),
            in_specs=[pl.BlockSpec(memory_space=pltpu.SMEM)] + [vmem] * 4,
            out_specs=vmem,
            scratch_shapes=[
                pltpu.VMEM((nr * nc, n + 16, width), jnp.bfloat16),
                pltpu.VMEM((nv, nt), jnp.float32),
                pltpu.VMEM((3, nv, LANES), jnp.bfloat16),
                pltpu.VMEM((nv, LANES), jnp.float32),
                pltpu.VMEM((ITERS + 1, 1, nt), jnp.float32),
                pltpu.VMEM((1, nt), jnp.float32),
                pltpu.VMEM((LANES, LANES), jnp.float32),
                pltpu.VMEM((ITERS, nc, 1, nt), jnp.float32),
                pltpu.VMEM((ITERS, nr, 1, nt), jnp.float32),
                dma, dma((nr,)), dma((nr, nc // 2)), dma((nr * (nc // 2),)), dma((nr * nc,)),
                dma((ITERS, nc)), dma((ITERS, nc)), dma((ITERS, nr)), dma((ITERS, nr)),
            ],
            compiler_params=pltpu.CompilerParams(
                collective_id=0, has_side_effects=True, vmem_limit_bytes=56 * 1024 * 1024),
            name="sinkhorn",
        )(level_cost, pair_level, block, valid_embed, valid_labels[None, :])
        return out.reshape(nt // nr)

    placed = (
        P(("row", "col"), None),
        P(("row", "col"), None),
        P(("row", "col")),
        P(("row", "col")),
        P(),
        P(),
    )
    return jax.shard_map(shards, mesh=mesh, in_specs=placed, out_specs=P("row"), check_vma=False)
```

```python
import functools
import math

import jax
import jax.numpy as jnp
from jax import lax
from jax.experimental import pallas as pl
from jax.experimental.pallas import tpu as pltpu
from jax.sharding import PartitionSpec as P

ITERS = 4
entropy_scale = 0.05
SCALE = math.log2(math.e) / entropy_scale
LOG2E = math.log2(math.e)
NT = (((1,), (1,)), ((), ()))
LANES = 128


def log2(x):
    return jnp.log(x) * LOG2E


def pieces(x, count):
    out = []
    for _ in range(count):
        part = x.astype(jnp.bfloat16)
        out.append(part)
        x = x - part.astype(jnp.float32)
    return out


def dot(a, b, dims=(((1,), (0,)), ((), ()))):
    return lax.dot_general(a, b, dims, preferred_element_type=jnp.float32)


def kernel(nr, nc, n, level_hbm, pair_hbm, block_ref, lab_ref, valid_hbm, vlab_hbm, out_ref,
           buf, labs, level_ref, pair_ref, valid_ref, vlab_ref,
           cost, y_ref, b_ref, a_ref, norm_ref, table_ref, part_ref, high_ref, pbuf, zbuf,
           local_sem, gsend, lsend, grecv, lrecv, psend, precv, zsend, zrecv):
    width = valid_ref.shape[1]
    nv = valid_ref.shape[0]
    nt = nr * nc * n
    nh = nc // 2
    kap = SCALE / width
    r = lax.axis_index("row")
    c = lax.axis_index("col")
    hi = c // 2
    lo = c % 2
    me = r * nc + c

    def rc(src, dst, ss, rs, row, col):
        return pltpu.make_async_remote_copy(
            src_ref=src, dst_ref=dst, send_sem=ss, recv_sem=rs,
            device_id={"row": row, "col": col}, device_id_type=pl.DeviceIdType.MESH)

    def loop(lower, upper, body):
        if upper - lower <= 8:
            for i in range(lower, upper):
                body(i)
        else:
            lax.fori_loop(lower, upper, lambda i, _: (body(i), 0)[1], 0)

    pairs = ((level_hbm, level_ref), (pair_hbm, pair_ref), (valid_hbm, valid_ref), (vlab_hbm, vlab_ref),
             (block_ref, buf.at[me]), (lab_ref, labs.at[me]))
    copies = [pltpu.make_async_copy(src, dst, local_sem.at[k]) for k, (src, dst) in enumerate(pairs)]
    for copy in copies:
        copy.start()

    barrier = pltpu.get_barrier_semaphore()
    loop(1, nr, lambda d: pl.semaphore_signal(
        barrier, inc=1, device_id={"row": (r + d) % nr, "col": c}, device_id_type=pl.DeviceIdType.MESH))
    loop(1, nc, lambda d: pl.semaphore_signal(
        barrier, inc=1, device_id={"row": r, "col": (c + d) % nc}, device_id_type=pl.DeviceIdType.MESH))
    pl.semaphore_wait(barrier, nr + nc - 2)

    square = nr == 4
    quad = nh == 4

    def flip(x, k):
        if k == 1:
            return x + 1 - 2 * (x % 2)
        return (x + 2) % 4 if k == 2 else 3 - x

    def row_to(d):
        return (flip(r, d) if d else r) if square else (r + d) % nr

    def row_from(d):
        return (flip(r, d) if d else r) if square else (r + nr - d) % nr

    def send(b, k, row, col, own):
        data = rc(block_ref if own else buf.at[b], buf.at[b], gsend.at[k], grecv.at[b], row, col)
        label = rc(lab_ref if own else labs.at[b], labs.at[b], lsend.at[k], lrecv.at[b], row, col)
        data.start()
        label.start()

    def sent(k):
        rc(block_ref, buf.at[me], gsend.at[k], grecv.at[me], r, hi * 2 + 1 - lo).wait_send()
        rc(lab_ref, labs.at[me], lsend.at[k], lrecv.at[me], r, hi * 2 + 1 - lo).wait_send()

    def arrived(b):
        rc(buf.at[b], buf.at[b], gsend.at[0], grecv.at[b], r, hi * 2 + 1 - lo).wait_recv()
        rc(labs.at[b], labs.at[b], lsend.at[0], lrecv.at[b], r, hi * 2 + 1 - lo).wait_recv()

    def block_id(d, high):
        return row_from(d) * nc + high * 2 + lo

    def to_plane(b, d, own):
        if quad:
            send(b, nr + d * nh + 1, r, flip(hi, 1) * 2 + lo, own)
            send(b, nr + d * nh + 2, r, flip(hi, 2) * 2 + lo, own)
        else:
            loop(1, nh, lambda e: send(b, nr + d * nh + e, r, ((hi + e) % nh) * 2 + lo, own))
        to_partner(b, d, 0, own)

    def to_partner(b, d, e, own):
        send(b, nr + nr * nh + d * nh + e, r, hi * 2 + 1 - lo, own)

    def from_row(d):
        b = block_id(d, hi)
        arrived(b)
        to_plane(b, d, False)

    def relay(d):
        if quad:
            near = flip(hi, 1) * (1 - lo) + flip(hi, 2) * lo
            side = flip(hi, 1) * lo + flip(hi, 2) * (1 - lo)
            b = block_id(d, near)
            arrived(b)
            send(b, nr + d * nh + 3, r, side * 2 + lo, False)
            to_partner(b, d, 1, False)
            for e, high in ((2, side), (3, 3 - hi)):
                b = block_id(d, high)
                arrived(b)
                to_partner(b, d, e, False)
        else:
            def one(e):
                b = block_id(d, (hi + nh - e) % nh)
                arrived(b)
                to_partner(b, d, e, False)
            loop(1, nh, one)

    def complete(d):
        loop(0, nh, lambda e: arrived(row_from(d) * nc + e * 2 + (1 - lo)))

    to_plane(me, 0, True)
    loop(1, nr, lambda d: send(me, d, row_to(d), c, True))

    for copy in copies:
        copy.wait()
    valid = valid_ref[...]
    wide = valid.astype(jnp.float32)
    b_ref[...] = jnp.broadcast_to(-kap * jnp.sum(wide * wide, axis=1, keepdims=True), b_ref.shape)
    classes = pair_ref.shape[0]
    pair = pair_ref[...]
    table = jnp.zeros(pair.shape, jnp.float32)
    for level in range(level_ref.shape[0]):
        table = table + jnp.where(pair == level, level_ref[level], 0.0)
    table_ref[...] = jnp.zeros_like(table_ref)
    table_ref[0:classes, 0:classes] = table * (-0.5 * width)
    hot = (lax.broadcasted_iota(jnp.int32, (LANES, nv), 0) == vlab_ref[...]).astype(jnp.float32)
    hot = hot.T.astype(jnp.bfloat16)
    for k, part in enumerate(pieces(table_ref[...], 3)):
        y_ref[k] = dot(hot, part, NT).astype(jnp.bfloat16)

    chunk = 256
    per = chunk // n
    ones = jnp.ones((8, width), jnp.bfloat16)

    def build_chunk(m):
        rows = buf[pl.ds(m * per, per)].reshape(chunk, width)
        labels = jnp.concatenate([labs[m * per + q] for q in range(per)], axis=1)
        ids = lax.broadcasted_iota(jnp.int32, (LANES, chunk), 0)
        t_hot = (ids == labels).astype(jnp.float32).astype(jnp.bfloat16)
        total = dot(valid_ref[...], rows, NT)
        for k in range(3):
            total = total + dot(y_ref[k], t_hot)
        at = pl.ds(pl.multiple_of(m * chunk, chunk), chunk)
        cost[:, at] = total * (2.0 * kap)
        wide = rows.astype(jnp.float32)
        high, low = pieces(wide * wide, 2)
        sq = dot(ones, high, NT) + dot(ones, low, NT)
        norm_ref[:, at] = sq[0:1] * kap
        row_part(0, at, chunk)

    def build(d):
        here = nc * n // chunk
        loop(0, here, lambda m: build_chunk(row_from(d) * here + m))

    def row_part(e, at, span):
        def term(k):
            rows = pl.ds(pl.multiple_of(k * 8, 8), 8)
            pot = b_ref[rows, :]
            return cost[rows, at] + jnp.concatenate([pot] * (span // LANES), axis=1)

        high = lax.fori_loop(0, nv // 8, lambda k, h: jnp.maximum(h, term(k)),
                             jnp.full((8, span), -jnp.inf, jnp.float32), unroll=8)
        high = jnp.max(high, axis=0, keepdims=True)
        wide_high = jnp.broadcast_to(high, (8, span))
        total = lax.fori_loop(0, nv // 8, lambda k, s: s + jnp.exp2(term(k) - wide_high),
                              jnp.zeros((8, span), jnp.float32), unroll=8)
        total = jnp.sum(total, axis=0, keepdims=True)
        pbuf[e, c, :, at] = high + log2(total)

    if square:
        from_row(1)
        relay(0)
        from_row(2)
        relay(1)
        complete(0)
        build(0)
        from_row(3)
        relay(2)
        complete(1)
        build(1)
        relay(3)
        complete(2)
        build(2)
        complete(3)
        build(3)
    else:
        loop(1, nr, from_row)
        loop(0, nr, relay)
        loop(0, nr, complete)
        loop(0, nr, build)
    a_ref[0] = -norm_ref[...]

    full_rows = nt
    full_cols = nv * nr * nc
    span = 512

    def row_side(e):
        for w in range(nt // span):
            row_part(e, slice(w * span, (w + 1) * span), span)

    def fold(op, values):
        while len(values) > 1:
            values = [op(*values[k:k + 2]) if k + 1 < len(values) else values[k]
                      for k in range(0, len(values), 2)]
        return values[0]

    def lanes(x):
        return [x[:, k:k + LANES] for k in range(0, x.shape[1], LANES)]

    def col_side(a):
        pot = jnp.broadcast_to(a, (8, nt))

        def highest(k, _):
            rows = pl.ds(pl.multiple_of(k * 8, 8), 8)
            part_ref[rows, :] = fold(jnp.maximum, lanes(cost[rows, :] + pot))
            return 0

        lax.fori_loop(0, nv // 8, highest, 0, unroll=4)
        high_ref[...] = jnp.broadcast_to(jnp.max(part_ref[...], axis=1, keepdims=True), high_ref.shape)

        def summed(k, _):
            rows = pl.ds(pl.multiple_of(k * 8, 8), 8)
            high = high_ref[rows, :]
            part_ref[rows, :] = fold(jnp.add, [jnp.exp2(x - high) for x in lanes(cost[rows, :] + pot)])
            return 0

        lax.fori_loop(0, nv // 8, summed, 0, unroll=4)
        total = jnp.broadcast_to(jnp.sum(part_ref[...], axis=1, keepdims=True), part_ref.shape)
        b_ref[...] = 0.5 * (b_ref[...] + (math.log2(full_rows) - (high_ref[...] + log2(total))))

    def p_copy(e, d, to):
        src = c if to else (c + nc - d) % nc
        return rc(pbuf.at[e, src], pbuf.at[e, src], psend.at[e, d], precv.at[e, d], r, (c + d) % nc)

    def z_copy(e, d, to):
        src = r if to else (r + nr - d) % nr
        return rc(zbuf.at[e, src], zbuf.at[e, src], zsend.at[e, d], zrecv.at[e, d], (r + d) % nr, c)

    def joined(parts):
        high = jnp.max(parts, axis=0)
        return high + log2(jnp.sum(jnp.exp2(parts - high[None]), axis=0))

    def send_plane(e):
        loop(1, nc, lambda d: p_copy(e, d, True).start())

    def turn(e):
        loop(1, nc, lambda d: p_copy(e, d, False).wait_recv())
        zbuf[e, r] = joined(pbuf[e])
        loop(1, nr, lambda d: z_copy(e, d, True).start())

    def finish(e):
        loop(1, nr, lambda d: z_copy(e, d, False).wait_recv())
        a_ref[e + 1] = 0.5 * (a_ref[e] + (math.log2(full_cols) - joined(zbuf[e])))

    send_plane(0)
    col_side(a_ref[0])
    row_side(1)
    send_plane(1)
    for e in range(0, ITERS, 2):
        turn(e)
        turn(e + 1)
        finish(e)
        if e + 2 < ITERS:
            col_side(a_ref[e + 1])
            row_side(e + 2)
            send_plane(e + 2)
        finish(e + 1)
        if e + 3 < ITERS:
            col_side(a_ref[e + 2])
            row_side(e + 3)
            send_plane(e + 3)

    row_pot = (a_ref[ITERS] + norm_ref[...]) * (1.0 / SCALE)
    result = (row_pot * full_rows - jnp.sum(row_pot, axis=1, keepdims=True)) * (1.0 / (full_rows - 1))
    norm_ref[...] = result
    span_out = nt // nr
    out_ref[...] = norm_ref[:, pl.ds(pl.multiple_of(r * span_out, span_out), span_out)]

    loop(1, nr, sent)
    loop(0, nr, lambda d: loop(1, nh, lambda e: sent(nr + d * nh + e)))
    loop(0, nr, lambda d: loop(0, nh, lambda e: sent(nr + nr * nh + d * nh + e)))
    for e in range(ITERS):
        loop(1, nc, lambda d: p_copy(e, d, True).wait_send())
        loop(1, nr, lambda d: z_copy(e, d, True).wait_send())


def solution(mesh):
    nr, nc = mesh.shape["row"], mesh.shape["col"]

    def shards(train_embed, valid_embed, train_labels, valid_labels, pair_level, level_cost):
        n, width = train_embed.shape
        nv = valid_embed.shape[0]
        nt = nr * nc * n
        vmem = pl.BlockSpec(memory_space=pltpu.VMEM)
        dma = pltpu.SemaphoreType.DMA
        sends = nr + nr * nc
        out = pl.pallas_call(
            functools.partial(kernel, nr, nc, n),
            out_shape=jax.ShapeDtypeStruct((1, nt // nr), jnp.float32),
            in_specs=[pl.BlockSpec(memory_space=pl.ANY)] * 6,
            out_specs=vmem,
            scratch_shapes=[
                pltpu.VMEM((nr * nc, n, width), jnp.bfloat16),
                pltpu.VMEM((nr * nc, 1, n), jnp.int32),
                pltpu.SMEM(level_cost.shape, jnp.float32),
                pltpu.VMEM(pair_level.shape, jnp.int32),
                pltpu.VMEM((nv, width), jnp.bfloat16),
                pltpu.VMEM((1, nv), jnp.int32),
                pltpu.VMEM((nv, nt), jnp.float32),
                pltpu.VMEM((3, nv, LANES), jnp.bfloat16),
                pltpu.VMEM((nv, LANES), jnp.float32),
                pltpu.VMEM((ITERS + 1, 1, nt), jnp.float32),
                pltpu.VMEM((1, nt), jnp.float32),
                pltpu.VMEM((LANES, LANES), jnp.float32),
                pltpu.VMEM((nv, LANES), jnp.float32),
                pltpu.VMEM((nv, LANES), jnp.float32),
                pltpu.VMEM((ITERS, nc, 1, nt), jnp.float32),
                pltpu.VMEM((ITERS, nr, 1, nt), jnp.float32),
                dma((6,)), dma((sends,)), dma((sends,)), dma((nr * nc,)), dma((nr * nc,)),
                dma((ITERS, nc)), dma((ITERS, nc)), dma((ITERS, nr)), dma((ITERS, nr)),
            ],
            compiler_params=pltpu.CompilerParams(
                collective_id=0, has_side_effects=True, vmem_limit_bytes=56 * 1024 * 1024),
            name="sinkhorn",
        )(level_cost, pair_level, train_embed, train_labels[None, :], valid_embed, valid_labels[None, :])
        return out.reshape(nt // nr)

    placed = (
        P(("row", "col"), None),
        P(("row", "col"), None),
        P(("row", "col")),
        P(("row", "col")),
        P(),
        P(),
    )
    return jax.shard_map(shards, mesh=mesh, in_specs=placed, out_specs=P("row"), check_vma=False)
```

```python
import functools
import math

import jax
import jax.numpy as jnp
from jax import lax
from jax.experimental import pallas as pl
from jax.experimental.pallas import tpu as pltpu
from jax.sharding import PartitionSpec as P

ITERS = 4
entropy_scale = 0.05
SCALE = math.log2(math.e) / entropy_scale
LOG2E = math.log2(math.e)
NT = (((1,), (1,)), ((), ()))
LANES = 128


def log2(x):
    return jnp.log(x) * LOG2E


def pieces(x, count):
    out = []
    for _ in range(count):
        part = x.astype(jnp.bfloat16)
        out.append(part)
        x = x - part.astype(jnp.float32)
    return out


def dot(a, b, dims=(((1,), (0,)), ((), ()))):
    return lax.dot_general(a, b, dims, preferred_element_type=jnp.float32)


def kernel(nr, nc, n, level_hbm, pair_hbm, block_ref, lab_hbm, valid_hbm, vlab_hbm, out_ref,
           buf, labs, lab_ref, level_ref, pair_ref, valid_ref, vlab_ref,
           cost, y_ref, b_ref, a_ref, norm_ref, table_ref, part_ref, high_ref, pbuf, zbuf,
           local_sem, gsend, lsend, grecv, lrecv, psend, precv, zsend, zrecv):
    width = valid_ref.shape[1]
    nv = valid_ref.shape[0]
    nt = nr * nc * n
    nh = nc // 2
    kap = SCALE / width
    r = lax.axis_index("row")
    c = lax.axis_index("col")
    hi = c // 2
    lo = c % 2
    me = r * nc + c

    def rc(src, dst, ss, rs, row, col):
        return pltpu.make_async_remote_copy(
            src_ref=src, dst_ref=dst, send_sem=ss, recv_sem=rs,
            device_id={"row": row, "col": col}, device_id_type=pl.DeviceIdType.MESH)

    def loop(lower, upper, body):
        if upper - lower <= 8:
            for i in range(lower, upper):
                body(i)
        else:
            lax.fori_loop(lower, upper, lambda i, _: (body(i), 0)[1], 0)

    pairs = ((level_hbm, level_ref), (pair_hbm, pair_ref), (valid_hbm, valid_ref), (vlab_hbm, vlab_ref),
             (block_ref, buf.at[me]), (lab_hbm, lab_ref))
    copies = [pltpu.make_async_copy(src, dst, local_sem.at[k]) for k, (src, dst) in enumerate(pairs)]
    for copy in copies:
        copy.start()

    barrier = pltpu.get_barrier_semaphore()
    loop(1, nr, lambda d: pl.semaphore_signal(
        barrier, inc=1, device_id={"row": (r + d) % nr, "col": c}, device_id_type=pl.DeviceIdType.MESH))
    loop(1, nc, lambda d: pl.semaphore_signal(
        barrier, inc=1, device_id={"row": r, "col": (c + d) % nc}, device_id_type=pl.DeviceIdType.MESH))
    for copy in copies[4:]:
        copy.wait()
    wide = buf[me].astype(jnp.float32)
    wide = jnp.sum(wide * wide, axis=1, keepdims=True) * kap
    mine = lax.broadcasted_iota(jnp.int32, (n, n), 0) == lax.broadcasted_iota(jnp.int32, (n, n), 1)
    labs[me, 0:1, :] = lab_ref[...].astype(jnp.float32)
    labs[me, 1:2, :] = jnp.sum(jnp.where(mine, wide, 0.0), axis=0, keepdims=True)
    pl.semaphore_wait(barrier, nr + nc - 2)

    square = nr == 4

    def flip(x, k):
        if k == 1:
            return x + 1 - 2 * (x % 2)
        return (x + 2) % 4 if k == 2 else 3 - x

    def row_to(d):
        return (flip(r, d) if d else r) if square else (r + d) % nr

    def row_from(d):
        return (flip(r, d) if d else r) if square else (r + nr - d) % nr

    def send(b, k, row, col, own):
        data = rc(block_ref if own else buf.at[b], buf.at[b], gsend.at[k], grecv.at[b], row, col)
        label = rc(labs.at[b], labs.at[b], lsend.at[k], lrecv.at[b], row, col)
        data.start()
        label.start()

    def sent(k):
        rc(block_ref, buf.at[me], gsend.at[k], grecv.at[me], r, hi * 2 + 1 - lo).wait_send()
        rc(labs.at[me], labs.at[me], lsend.at[k], lrecv.at[me], r, hi * 2 + 1 - lo).wait_send()

    def arrived(b):
        rc(buf.at[b], buf.at[b], gsend.at[0], grecv.at[b], r, hi * 2 + 1 - lo).wait_recv()
        rc(labs.at[b], labs.at[b], lsend.at[0], lrecv.at[b], r, hi * 2 + 1 - lo).wait_recv()

    def block_id(d, high):
        return row_from(d) * nc + high * 2 + lo

    def to_plane(b, d, own):
        loop(1, nh, lambda e: send(b, nr + d * nh + e, r, ((hi + e) % nh) * 2 + lo, own))
        to_partner(b, d, 0, own)

    def to_partner(b, d, e, own):
        send(b, nr + nr * nh + d * nh + e, r, hi * 2 + 1 - lo, own)

    def from_row(d):
        b = block_id(d, hi)
        arrived(b)
        to_plane(b, d, False)

    def relay(d):
        def one(e):
            b = block_id(d, (hi + nh - e) % nh)
            arrived(b)
            to_partner(b, d, e, False)
        loop(1, nh, one)

    def complete(d):
        loop(0, nh, lambda e: arrived(row_from(d) * nc + e * 2 + (1 - lo)))

    to_plane(me, 0, True)
    loop(1, nr, lambda d: send(me, d, row_to(d), c, True))

    for copy in copies[:4]:
        copy.wait()
    valid = valid_ref[...]
    wide = valid.astype(jnp.float32)
    b_ref[...] = jnp.broadcast_to(-kap * jnp.sum(wide * wide, axis=1, keepdims=True), b_ref.shape)
    classes = pair_ref.shape[0]
    pair = pair_ref[...]
    table = jnp.zeros(pair.shape, jnp.float32)
    for level in range(level_ref.shape[0]):
        table = table + jnp.where(pair == level, level_ref[level], 0.0)
    table_ref[...] = jnp.zeros_like(table_ref)
    table_ref[0:classes, 0:classes] = table * (-0.5 * width)
    hot = (lax.broadcasted_iota(jnp.int32, (LANES, nv), 0) == vlab_ref[...]).astype(jnp.float32)
    hot = hot.T.astype(jnp.bfloat16)
    for k, part in enumerate(pieces(table_ref[...], 3)):
        y_ref[:, k * LANES:(k + 1) * LANES] = dot(hot, part, NT).astype(jnp.bfloat16)

    chunk = 256
    per = chunk // n

    def build_chunk(m):
        rows = buf[pl.ds(m * per, per)].reshape(chunk, width)
        labels = jnp.concatenate([labs[m * per + q] for q in range(per)], axis=1)
        ids = lax.broadcasted_iota(jnp.int32, (LANES, chunk), 0)
        t_hot = (ids == labels[0:1].astype(jnp.int32)).astype(jnp.float32).astype(jnp.bfloat16)
        total = dot(valid_ref[...], rows, NT) + dot(y_ref[...], jnp.concatenate([t_hot] * 3, axis=0))
        at = pl.ds(pl.multiple_of(m * chunk, chunk), chunk)
        cost[:, at] = total * (2.0 * kap)
        norm_ref[:, at] = labels[1:2]

    def build(d):
        here = nc * n // chunk
        loop(0, here, lambda m: build_chunk(row_from(d) * here + m))
        row_part(0, pl.ds(pl.multiple_of(row_from(d) * here * chunk, chunk), here * chunk), here * chunk)

    def fold(op, values):
        while len(values) > 1:
            values = [op(*values[k:k + 2]) if k + 1 < len(values) else values[k]
                      for k in range(0, len(values), 2)]
        return values[0]

    def row_part(e, at, span):
        def term(k):
            rows = pl.ds(pl.multiple_of(k * 8, 8), 8)
            pot = b_ref[rows, :]
            return cost[rows, at] + jnp.concatenate([pot] * (span // LANES), axis=1)

        def sweep(op, start, value):
            step = math.gcd(nv // 8, 8)

            def body(k, state):
                return op(state, fold(op, [value(k * step + q) for q in range(step)]))

            return lax.fori_loop(0, nv // 8 // step, body, jnp.full((8, span), start, jnp.float32), unroll=2)

        high = jnp.max(sweep(jnp.maximum, -jnp.inf, term), axis=0, keepdims=True)
        wide_high = jnp.broadcast_to(high, (8, span))
        total = sweep(jnp.add, 0.0, lambda k: jnp.exp2(term(k) - wide_high))
        total = jnp.sum(total, axis=0, keepdims=True)
        pbuf[e, c, :, at] = high + log2(total)

    if square:
        from_row(1)
        from_row(2)
        relay(0)
        from_row(3)
        relay(1)
        complete(0)
        build(0)
        relay(2)
        complete(1)
        build(1)
        relay(3)
        complete(2)
        build(2)
        complete(3)
        build(3)
    else:
        loop(1, nr, from_row)
        loop(0, nr, relay)
        loop(0, nr, complete)
        loop(0, nr, build)
    a_ref[0] = -norm_ref[...]

    full_rows = nt
    full_cols = nv * nr * nc
    span = 512

    def row_side(e):
        for w in range(nt // span):
            row_part(e, slice(w * span, (w + 1) * span), span)

    def lanes(x):
        return [x[:, k:k + LANES] for k in range(0, x.shape[1], LANES)]

    def col_side(a):
        pot = jnp.broadcast_to(a, (8, nt))

        def highest(k, _):
            rows = pl.ds(pl.multiple_of(k * 8, 8), 8)
            part_ref[rows, :] = fold(jnp.maximum, lanes(cost[rows, :] + pot))
            return 0

        lax.fori_loop(0, nv // 8, highest, 0, unroll=4)
        high_ref[...] = jnp.broadcast_to(jnp.max(part_ref[...], axis=1, keepdims=True), high_ref.shape)

        def summed(k, _):
            rows = pl.ds(pl.multiple_of(k * 8, 8), 8)
            high = high_ref[rows, :]
            part_ref[rows, :] = fold(jnp.add, [jnp.exp2(x - high) for x in lanes(cost[rows, :] + pot)])
            return 0

        lax.fori_loop(0, nv // 8, summed, 0, unroll=4)
        total = jnp.broadcast_to(jnp.sum(part_ref[...], axis=1, keepdims=True), part_ref.shape)
        b_ref[...] = 0.5 * (b_ref[...] + (math.log2(full_rows) - (high_ref[...] + log2(total))))

    def p_copy(e, d, to):
        src = c if to else (c + nc - d) % nc
        return rc(pbuf.at[e, src], pbuf.at[e, src], psend.at[e, d], precv.at[e, d], r, (c + d) % nc)

    def z_copy(e, d, to):
        src = r if to else (r + nr - d) % nr
        return rc(zbuf.at[e, src], zbuf.at[e, src], zsend.at[e, d], zrecv.at[e, d], (r + d) % nr, c)

    def joined(parts):
        high = jnp.max(parts, axis=0)
        return high + log2(jnp.sum(jnp.exp2(parts - high[None]), axis=0))

    def send_plane(e):
        loop(1, nc, lambda d: p_copy(e, d, True).start())

    def turn(e):
        loop(1, nc, lambda d: p_copy(e, d, False).wait_recv())
        zbuf[e, r] = joined(pbuf[e])
        loop(1, nr, lambda d: z_copy(e, d, True).start())

    def finish(e):
        loop(1, nr, lambda d: z_copy(e, d, False).wait_recv())
        a_ref[e + 1] = 0.5 * (a_ref[e] + (math.log2(full_cols) - joined(zbuf[e])))

    send_plane(0)
    col_side(a_ref[0])
    row_side(1)
    send_plane(1)
    for e in range(0, ITERS, 2):
        turn(e)
        turn(e + 1)
        finish(e)
        if e + 2 < ITERS:
            col_side(a_ref[e + 1])
            row_side(e + 2)
            send_plane(e + 2)
        finish(e + 1)
        if e + 3 < ITERS:
            col_side(a_ref[e + 2])
            row_side(e + 3)
            send_plane(e + 3)

    row_pot = (a_ref[ITERS] + norm_ref[...]) * (1.0 / SCALE)
    result = (row_pot * full_rows - jnp.sum(row_pot, axis=1, keepdims=True)) * (1.0 / (full_rows - 1))
    norm_ref[...] = result
    span_out = nt // nr
    out_ref[...] = norm_ref[:, pl.ds(pl.multiple_of(r * span_out, span_out), span_out)]

    loop(1, nr, sent)
    loop(0, nr, lambda d: loop(1, nh, lambda e: sent(nr + d * nh + e)))
    loop(0, nr, lambda d: loop(0, nh, lambda e: sent(nr + nr * nh + d * nh + e)))
    for e in range(ITERS):
        loop(1, nc, lambda d: p_copy(e, d, True).wait_send())
        loop(1, nr, lambda d: z_copy(e, d, True).wait_send())


def solution(mesh):
    nr, nc = mesh.shape["row"], mesh.shape["col"]

    def shards(train_embed, valid_embed, train_labels, valid_labels, pair_level, level_cost):
        n, width = train_embed.shape
        nv = valid_embed.shape[0]
        nt = nr * nc * n
        vmem = pl.BlockSpec(memory_space=pltpu.VMEM)
        dma = pltpu.SemaphoreType.DMA
        sends = nr + nr * nc
        out = pl.pallas_call(
            functools.partial(kernel, nr, nc, n),
            out_shape=jax.ShapeDtypeStruct((1, nt // nr), jnp.float32),
            in_specs=[pl.BlockSpec(memory_space=pl.ANY)] * 6,
            out_specs=vmem,
            scratch_shapes=[
                pltpu.VMEM((nr * nc, n, width), jnp.bfloat16),
                pltpu.VMEM((nr * nc, 2, n), jnp.float32),
                pltpu.VMEM((1, n), jnp.int32),
                pltpu.SMEM(level_cost.shape, jnp.float32),
                pltpu.VMEM(pair_level.shape, jnp.int32),
                pltpu.VMEM((nv, width), jnp.bfloat16),
                pltpu.VMEM((1, nv), jnp.int32),
                pltpu.VMEM((nv, nt), jnp.float32),
                pltpu.VMEM((nv, 3 * LANES), jnp.bfloat16),
                pltpu.VMEM((nv, LANES), jnp.float32),
                pltpu.VMEM((ITERS + 1, 1, nt), jnp.float32),
                pltpu.VMEM((1, nt), jnp.float32),
                pltpu.VMEM((LANES, LANES), jnp.float32),
                pltpu.VMEM((nv, LANES), jnp.float32),
                pltpu.VMEM((nv, LANES), jnp.float32),
                pltpu.VMEM((ITERS, nc, 1, nt), jnp.float32),
                pltpu.VMEM((ITERS, nr, 1, nt), jnp.float32),
                dma((6,)), dma((sends,)), dma((sends,)), dma((nr * nc,)), dma((nr * nc,)),
                dma((ITERS, nc)), dma((ITERS, nc)), dma((ITERS, nr)), dma((ITERS, nr)),
            ],
            compiler_params=pltpu.CompilerParams(
                collective_id=0, has_side_effects=True, vmem_limit_bytes=56 * 1024 * 1024),
            name="sinkhorn",
        )(level_cost, pair_level, train_embed, train_labels[None, :], valid_embed, valid_labels[None, :])
        return out.reshape(nt // nr)

    placed = (
        P(("row", "col"), None),
        P(("row", "col"), None),
        P(("row", "col")),
        P(("row", "col")),
        P(),
        P(),
    )
    return jax.shard_map(shards, mesh=mesh, in_specs=placed, out_specs=P("row"), check_vma=False)
```

```python
import functools
import math

import jax
import jax.numpy as jnp
from jax import lax
from jax.experimental import pallas as pl
from jax.experimental.pallas import tpu as pltpu
from jax.sharding import PartitionSpec as P

ITERS = 4
entropy_scale = 0.05
SCALE = math.log2(math.e) / entropy_scale
LOG2E = math.log2(math.e)
NT = (((1,), (1,)), ((), ()))
LANES = 128


def log2(x):
    return jnp.log(x) * LOG2E


def pieces(x, count):
    out = []
    for _ in range(count):
        part = x.astype(jnp.bfloat16)
        out.append(part)
        x = x - part.astype(jnp.float32)
    return out


def dot(a, b, dims=(((1,), (0,)), ((), ()))):
    return lax.dot_general(a, b, dims, preferred_element_type=jnp.float32)


def kernel(nr, nc, n, level_hbm, pair_hbm, block_ref, lab_hbm, valid_hbm, vlab_hbm, out_ref,
           buf, labs, lab_ref, level_ref, pair_ref, valid_ref, vlab_ref,
           cost, y_ref, b_ref, a_ref, norm_ref, table_ref, part_ref, high_ref, pbuf, zbuf,
           local_sem, gsend, lsend, grecv, lrecv, psend, precv, zsend, zrecv):
    width = valid_ref.shape[1]
    nv = valid_ref.shape[0]
    nt = nr * nc * n
    nh = nc // 2
    kap = SCALE / width
    r = lax.axis_index("row")
    c = lax.axis_index("col")
    hi = c // 2
    lo = c % 2
    me = r * nc + c

    def rc(src, dst, ss, rs, row, col):
        return pltpu.make_async_remote_copy(
            src_ref=src, dst_ref=dst, send_sem=ss, recv_sem=rs,
            device_id={"row": row, "col": col}, device_id_type=pl.DeviceIdType.MESH)

    def loop(lower, upper, body):
        if upper - lower <= 8:
            for i in range(lower, upper):
                body(i)
        else:
            lax.fori_loop(lower, upper, lambda i, _: (body(i), 0)[1], 0)

    pairs = ((level_hbm, level_ref), (pair_hbm, pair_ref), (valid_hbm, valid_ref), (vlab_hbm, vlab_ref),
             (block_ref, buf.at[me]), (lab_hbm, lab_ref))
    copies = [pltpu.make_async_copy(src, dst, local_sem.at[k]) for k, (src, dst) in enumerate(pairs)]
    for copy in copies:
        copy.start()

    barrier = pltpu.get_barrier_semaphore()
    loop(1, nr, lambda d: pl.semaphore_signal(
        barrier, inc=1, device_id={"row": (r + d) % nr, "col": c}, device_id_type=pl.DeviceIdType.MESH))
    loop(1, nc, lambda d: pl.semaphore_signal(
        barrier, inc=1, device_id={"row": r, "col": (c + d) % nc}, device_id_type=pl.DeviceIdType.MESH))
    for copy in copies[4:]:
        copy.wait()
    wide = buf[me].astype(jnp.float32)
    wide = jnp.sum(wide * wide, axis=1, keepdims=True) * kap
    mine = lax.broadcasted_iota(jnp.int32, (n, n), 0) == lax.broadcasted_iota(jnp.int32, (n, n), 1)
    labs[me, 0:1, :] = lab_ref[...].astype(jnp.float32)
    labs[me, 1:2, :] = jnp.sum(jnp.where(mine, wide, 0.0), axis=0, keepdims=True)
    pl.semaphore_wait(barrier, nr + nc - 2)

    square = nr == 4

    def flip(x, k):
        if k == 1:
            return x + 1 - 2 * (x % 2)
        return (x + 2) % 4 if k == 2 else 3 - x

    def row_to(d):
        return (flip(r, d) if d else r) if square else (r + d) % nr

    def row_from(d):
        return (flip(r, d) if d else r) if square else (r + nr - d) % nr

    def send(b, k, row, col, own):
        data = rc(block_ref if own else buf.at[b], buf.at[b], gsend.at[k], grecv.at[b], row, col)
        label = rc(labs.at[b], labs.at[b], lsend.at[k], lrecv.at[b], row, col)
        data.start()
        label.start()

    def sent(k):
        rc(block_ref, buf.at[me], gsend.at[k], grecv.at[me], r, hi * 2 + 1 - lo).wait_send()
        rc(labs.at[me], labs.at[me], lsend.at[k], lrecv.at[me], r, hi * 2 + 1 - lo).wait_send()

    def arrived(b):
        rc(buf.at[b], buf.at[b], gsend.at[0], grecv.at[b], r, hi * 2 + 1 - lo).wait_recv()
        rc(labs.at[b], labs.at[b], lsend.at[0], lrecv.at[b], r, hi * 2 + 1 - lo).wait_recv()

    def block_id(d, high):
        return row_from(d) * nc + high * 2 + lo

    def to_plane(b, d, own):
        loop(1, nh, lambda e: send(b, nr + d * nh + e, r, ((hi + e) % nh) * 2 + lo, own))
        to_partner(b, d, 0, own)

    def to_partner(b, d, e, own):
        send(b, nr + nr * nh + d * nh + e, r, hi * 2 + 1 - lo, own)

    def from_row(d):
        b = block_id(d, hi)
        arrived(b)
        to_plane(b, d, False)

    def relay(d):
        def one(e):
            b = block_id(d, (hi + nh - e) % nh)
            arrived(b)
            to_partner(b, d, e, False)
        loop(1, nh, one)

    def complete(d):
        loop(0, nh, lambda e: arrived(row_from(d) * nc + e * 2 + (1 - lo)))

    to_plane(me, 0, True)
    loop(1, nr, lambda d: send(me, d, row_to(d), c, True))

    for copy in copies[:4]:
        copy.wait()
    valid = valid_ref[...]
    wide = valid.astype(jnp.float32)
    b_ref[...] = jnp.broadcast_to(-kap * jnp.sum(wide * wide, axis=1, keepdims=True), b_ref.shape)
    classes = pair_ref.shape[0]
    pair = pair_ref[...]
    table = jnp.zeros(pair.shape, jnp.float32)
    for level in range(level_ref.shape[0]):
        table = table + jnp.where(pair == level, level_ref[level], 0.0)
    table_ref[...] = jnp.zeros_like(table_ref)
    table_ref[0:classes, 0:classes] = table * (-0.5 * width)
    hot = (lax.broadcasted_iota(jnp.int32, (LANES, nv), 0) == vlab_ref[...]).astype(jnp.float32)
    hot = hot.T.astype(jnp.bfloat16)
    for k, part in enumerate(pieces(table_ref[...], 3)):
        y_ref[:, k * LANES:(k + 1) * LANES] = dot(hot, part, NT).astype(jnp.bfloat16)

    chunk = 256
    per = chunk // n

    def build_chunk(m):
        rows = buf[pl.ds(m * per, per)].reshape(chunk, width)
        labels = jnp.concatenate([labs[m * per + q] for q in range(per)], axis=1)
        ids = lax.broadcasted_iota(jnp.int32, (LANES, chunk), 0)
        t_hot = (ids == labels[0:1].astype(jnp.int32)).astype(jnp.float32).astype(jnp.bfloat16)
        total = dot(valid_ref[...], rows, NT) + dot(y_ref[...], jnp.concatenate([t_hot] * 3, axis=0))
        at = pl.ds(pl.multiple_of(m * chunk, chunk), chunk)
        cost[:, at] = total * (2.0 * kap)
        norm_ref[:, at] = labels[1:2]

    def build(d):
        here = nc * n // chunk
        loop(0, here, lambda m: build_chunk(row_from(d) * here + m))
        row_part(0, pl.ds(pl.multiple_of(row_from(d) * here * chunk, chunk), here * chunk), here * chunk)

    def fold(op, values):
        while len(values) > 1:
            values = [op(*values[k:k + 2]) if k + 1 < len(values) else values[k]
                      for k in range(0, len(values), 2)]
        return values[0]

    def row_part(e, at, span):
        def term(k):
            rows = pl.ds(pl.multiple_of(k * 8, 8), 8)
            pot = b_ref[rows, :]
            return cost[rows, at] + jnp.concatenate([pot] * (span // LANES), axis=1)

        def sweep(op, start, value):
            step = math.gcd(nv // 8, 8)

            def body(k, state):
                return op(state, fold(op, [value(k * step + q) for q in range(step)]))

            return lax.fori_loop(0, nv // 8 // step, body, jnp.full((8, span), start, jnp.float32), unroll=2)

        high = jnp.max(sweep(jnp.maximum, -jnp.inf, term), axis=0, keepdims=True)
        wide_high = jnp.broadcast_to(high, (8, span))
        total = sweep(jnp.add, 0.0, lambda k: jnp.exp2(term(k) - wide_high))
        total = jnp.sum(total, axis=0, keepdims=True)
        pbuf[e, c, :, at] = high + log2(total)

    if square:
        from_row(1)
        from_row(2)
        relay(0)
        from_row(3)
        relay(1)
        complete(0)
        build(0)
        relay(2)
        complete(1)
        build(1)
        relay(3)
        complete(2)
        build(2)
        complete(3)
        build(3)
    else:
        loop(1, nr, from_row)
        loop(0, nr, relay)
        loop(0, nr, complete)
        loop(0, nr, build)
    a_ref[0] = -norm_ref[...]

    full_rows = nt
    full_cols = nv * nr * nc
    span = 512

    def row_side(e):
        for w in range(nt // span):
            row_part(e, slice(w * span, (w + 1) * span), span)

    def lanes(x):
        return [x[:, k:k + LANES] for k in range(0, x.shape[1], LANES)]

    def col_side(a):
        pot = jnp.broadcast_to(a, (8, nt))

        def highest(k, _):
            rows = pl.ds(pl.multiple_of(k * 8, 8), 8)
            part_ref[rows, :] = fold(jnp.maximum, lanes(cost[rows, :] + pot))
            return 0

        lax.fori_loop(0, nv // 8, highest, 0, unroll=4)
        high_ref[...] = jnp.broadcast_to(jnp.max(part_ref[...], axis=1, keepdims=True), high_ref.shape)

        def summed(k, _):
            rows = pl.ds(pl.multiple_of(k * 8, 8), 8)
            high = high_ref[rows, :]
            part_ref[rows, :] = fold(jnp.add, [jnp.exp2(x - high) for x in lanes(cost[rows, :] + pot)])
            return 0

        lax.fori_loop(0, nv // 8, summed, 0, unroll=4)
        total = jnp.broadcast_to(jnp.sum(part_ref[...], axis=1, keepdims=True), part_ref.shape)
        b_ref[...] = 0.5 * (b_ref[...] + (math.log2(full_rows) - (high_ref[...] + log2(total))))

    def p_copy(e, d, to):
        src = c if to else (c + nc - d) % nc
        return rc(pbuf.at[e, src], pbuf.at[e, src], psend.at[e, d], precv.at[e, d], r, (c + d) % nc)

    def z_copy(e, d, to):
        src = r if to else (r + nr - d) % nr
        return rc(zbuf.at[e, src], zbuf.at[e, src], zsend.at[e, d], zrecv.at[e, d], (r + d) % nr, c)

    def joined(parts):
        high = jnp.max(parts, axis=0)
        return high + log2(jnp.sum(jnp.exp2(parts - high[None]), axis=0))

    def send_plane(e):
        loop(1, nc, lambda d: p_copy(e, d, True).start())

    def turn(e):
        loop(1, nc, lambda d: p_copy(e, d, False).wait_recv())
        zbuf[e, r] = joined(pbuf[e])
        loop(1, nr, lambda d: z_copy(e, d, True).start())

    def finish(e):
        loop(1, nr, lambda d: z_copy(e, d, False).wait_recv())
        a_ref[e + 1] = 0.5 * (a_ref[e] + (math.log2(full_cols) - joined(zbuf[e])))

    send_plane(0)
    col_side(a_ref[0])
    row_side(1)
    send_plane(1)
    for e in range(0, ITERS, 2):
        turn(e)
        turn(e + 1)
        finish(e)
        if e + 2 < ITERS:
            col_side(a_ref[e + 1])
            row_side(e + 2)
            send_plane(e + 2)
        finish(e + 1)
        if e + 3 < ITERS:
            col_side(a_ref[e + 2])
            row_side(e + 3)
            send_plane(e + 3)

    row_pot = (a_ref[ITERS] + norm_ref[...]) * (1.0 / SCALE)
    result = (row_pot * full_rows - jnp.sum(row_pot, axis=1, keepdims=True)) * (1.0 / (full_rows - 1))
    norm_ref[...] = result
    span_out = nt // nr
    out_ref[...] = norm_ref[:, pl.ds(pl.multiple_of(r * span_out, span_out), span_out)]

    loop(1, nr, sent)
    loop(0, nr, lambda d: loop(1, nh, lambda e: sent(nr + d * nh + e)))
    loop(0, nr, lambda d: loop(0, nh, lambda e: sent(nr + nr * nh + d * nh + e)))
    for e in range(ITERS):
        loop(1, nc, lambda d: p_copy(e, d, True).wait_send())
        loop(1, nr, lambda d: z_copy(e, d, True).wait_send())


def solution(mesh):
    nr, nc = mesh.shape["row"], mesh.shape["col"]

    def shards(train_embed, valid_embed, train_labels, valid_labels, pair_level, level_cost):
        n, width = train_embed.shape
        nv = valid_embed.shape[0]
        nt = nr * nc * n
        vmem = pl.BlockSpec(memory_space=pltpu.VMEM)
        dma = pltpu.SemaphoreType.DMA
        sends = nr + nr * nc
        out = pl.pallas_call(
            functools.partial(kernel, nr, nc, n),
            out_shape=pltpu.VMEM((1, nt // nr), jnp.float32),
            in_specs=[pl.BlockSpec(memory_space=pl.ANY)] * 6,
            out_specs=vmem,
            scratch_shapes=[
                pltpu.VMEM((nr * nc, n, width), jnp.bfloat16),
                pltpu.VMEM((nr * nc, 2, n), jnp.float32),
                pltpu.VMEM((1, n), jnp.int32),
                pltpu.SMEM(level_cost.shape, jnp.float32),
                pltpu.VMEM(pair_level.shape, jnp.int32),
                pltpu.VMEM((nv, width), jnp.bfloat16),
                pltpu.VMEM((1, nv), jnp.int32),
                pltpu.VMEM((nv, nt), jnp.float32),
                pltpu.VMEM((nv, 3 * LANES), jnp.bfloat16),
                pltpu.VMEM((nv, LANES), jnp.float32),
                pltpu.VMEM((ITERS + 1, 1, nt), jnp.float32),
                pltpu.VMEM((1, nt), jnp.float32),
                pltpu.VMEM((LANES, LANES), jnp.float32),
                pltpu.VMEM((nv, LANES), jnp.float32),
                pltpu.VMEM((nv, LANES), jnp.float32),
                pltpu.VMEM((ITERS, nc, 1, nt), jnp.float32),
                pltpu.VMEM((ITERS, nr, 1, nt), jnp.float32),
                dma((6,)), dma((sends,)), dma((sends,)), dma((nr * nc,)), dma((nr * nc,)),
                dma((ITERS, nc)), dma((ITERS, nc)), dma((ITERS, nr)), dma((ITERS, nr)),
            ],
            compiler_params=pltpu.CompilerParams(
                collective_id=0, has_side_effects=True, vmem_limit_bytes=56 * 1024 * 1024),
            name="sinkhorn",
        )(level_cost, pair_level, train_embed, train_labels[None, :], valid_embed, valid_labels[None, :])
        return out.reshape(nt // nr)

    placed = (
        P(("row", "col"), None),
        P(("row", "col"), None),
        P(("row", "col")),
        P(("row", "col")),
        P(),
        P(),
    )
    return jax.shard_map(shards, mesh=mesh, in_specs=placed, out_specs=P("row"), check_vma=False)
```

```python
import functools
import math

import jax
import jax.numpy as jnp
from jax import lax
from jax.experimental import pallas as pl
from jax.experimental.pallas import tpu as pltpu
from jax.sharding import PartitionSpec as P

ITERS = 4
entropy_scale = 0.05
SCALE = math.log2(math.e) / entropy_scale
LOG2E = math.log2(math.e)
NT = (((1,), (1,)), ((), ()))
LANES = 128


def log2(x):
    return jnp.log(x) * LOG2E


def pieces(x, count):
    out = []
    for _ in range(count):
        part = x.astype(jnp.bfloat16)
        out.append(part)
        x = x - part.astype(jnp.float32)
    return out


def dot(a, b, dims=(((1,), (0,)), ((), ()))):
    return lax.dot_general(a, b, dims, preferred_element_type=jnp.float32)


def kernel(nr, nc, n, level_hbm, pair_hbm, block_ref, lab_hbm, valid_hbm, vlab_hbm, out_ref,
           buf, labs, lab_ref, level_ref, pair_ref, valid_ref, vlab_ref,
           cost, y_ref, b_ref, a_ref, norm_ref, table_ref, part_ref, high_ref, pbuf, zbuf,
           local_sem, gsend, lsend, grecv, lrecv, psend, precv, zsend, zrecv):
    width = valid_ref.shape[1]
    nv = valid_ref.shape[0]
    nt = nr * nc * n
    nh = nc // 2
    kap = SCALE / width
    r = lax.axis_index("row")
    c = lax.axis_index("col")
    hi = c // 2
    lo = c % 2
    me = r * nc + c

    def rc(src, dst, ss, rs, row, col):
        return pltpu.make_async_remote_copy(
            src_ref=src, dst_ref=dst, send_sem=ss, recv_sem=rs,
            device_id={"row": row, "col": col}, device_id_type=pl.DeviceIdType.MESH)

    def loop(lower, upper, body):
        if upper - lower <= 8:
            for i in range(lower, upper):
                body(i)
        else:
            lax.fori_loop(lower, upper, lambda i, _: (body(i), 0)[1], 0)

    pairs = ((level_hbm, level_ref), (pair_hbm, pair_ref), (valid_hbm, valid_ref), (vlab_hbm, vlab_ref),
             (block_ref, buf.at[me]), (lab_hbm, lab_ref))
    copies = [pltpu.make_async_copy(src, dst, local_sem.at[k]) for k, (src, dst) in enumerate(pairs)]
    for copy in copies:
        copy.start()

    barrier = pltpu.get_barrier_semaphore()
    loop(1, nr, lambda d: pl.semaphore_signal(
        barrier, inc=1, device_id={"row": (r + d) % nr, "col": c}, device_id_type=pl.DeviceIdType.MESH))
    loop(1, nc, lambda d: pl.semaphore_signal(
        barrier, inc=1, device_id={"row": r, "col": (c + d) % nc}, device_id_type=pl.DeviceIdType.MESH))
    for copy in copies[4:]:
        copy.wait()
    wide = buf[me].astype(jnp.float32)
    wide = jnp.sum(wide * wide, axis=1, keepdims=True) * kap
    mine = lax.broadcasted_iota(jnp.int32, (n, n), 0) == lax.broadcasted_iota(jnp.int32, (n, n), 1)
    labs[me, 0:1, :] = lab_ref[...].astype(jnp.float32)
    labs[me, 1:2, :] = jnp.sum(jnp.where(mine, wide, 0.0), axis=0, keepdims=True)
    pl.semaphore_wait(barrier, nr + nc - 2)

    square = nr == 4

    def flip(x, k):
        if k == 1:
            return x + 1 - 2 * (x % 2)
        return (x + 2) % 4 if k == 2 else 3 - x

    def row_to(d):
        return (flip(r, d) if d else r) if square else (r + d) % nr

    def row_from(d):
        return (flip(r, d) if d else r) if square else (r + nr - d) % nr

    def send(b, k, row, col, own):
        data = rc(block_ref if own else buf.at[b], buf.at[b], gsend.at[k], grecv.at[b], row, col)
        label = rc(labs.at[b], labs.at[b], lsend.at[k], lrecv.at[b], row, col)
        data.start()
        label.start()

    def sent(k):
        rc(block_ref, buf.at[me], gsend.at[k], grecv.at[me], r, hi * 2 + 1 - lo).wait_send()
        rc(labs.at[me], labs.at[me], lsend.at[k], lrecv.at[me], r, hi * 2 + 1 - lo).wait_send()

    def arrived(b):
        rc(buf.at[b], buf.at[b], gsend.at[0], grecv.at[b], r, hi * 2 + 1 - lo).wait_recv()
        rc(labs.at[b], labs.at[b], lsend.at[0], lrecv.at[b], r, hi * 2 + 1 - lo).wait_recv()

    def block_id(d, high):
        return row_from(d) * nc + high * 2 + lo

    def to_plane(b, d, own):
        loop(1, nh, lambda e: send(b, nr + d * nh + e, r, ((hi + e) % nh) * 2 + lo, own))
        to_partner(b, d, 0, own)

    def to_partner(b, d, e, own):
        send(b, nr + nr * nh + d * nh + e, r, hi * 2 + 1 - lo, own)

    def from_row(d):
        b = block_id(d, hi)
        arrived(b)
        to_plane(b, d, False)

    def relay(d):
        def one(e):
            b = block_id(d, (hi + nh - e) % nh)
            arrived(b)
            to_partner(b, d, e, False)
        loop(1, nh, one)

    def complete(d):
        loop(0, nh, lambda e: arrived(row_from(d) * nc + e * 2 + (1 - lo)))

    to_plane(me, 0, True)
    loop(1, nr, lambda d: send(me, d, row_to(d), c, True))

    for copy in copies[:4]:
        copy.wait()
    valid = valid_ref[...]
    wide = valid.astype(jnp.float32)
    b_ref[...] = jnp.broadcast_to(-kap * jnp.sum(wide * wide, axis=1, keepdims=True), b_ref.shape)
    classes = pair_ref.shape[0]
    pair = pair_ref[...]
    table = jnp.zeros(pair.shape, jnp.float32)
    for level in range(level_ref.shape[0]):
        table = table + jnp.where(pair == level, level_ref[level], 0.0)
    table_ref[...] = jnp.zeros_like(table_ref)
    table_ref[0:classes, 0:classes] = table * (-0.5 * width)
    hot = (lax.broadcasted_iota(jnp.int32, (LANES, nv), 0) == vlab_ref[...]).astype(jnp.float32)
    hot = hot.T.astype(jnp.bfloat16)
    for k, part in enumerate(pieces(table_ref[...], 3)):
        y_ref[:, k * LANES:(k + 1) * LANES] = dot(hot, part, NT).astype(jnp.bfloat16)

    chunk = 256
    per = chunk // n

    def build_chunk(m):
        rows = buf[pl.ds(m * per, per)].reshape(chunk, width)
        labels = jnp.concatenate([labs[m * per + q] for q in range(per)], axis=1)
        ids = lax.broadcasted_iota(jnp.int32, (LANES, chunk), 0)
        t_hot = (ids == labels[0:1].astype(jnp.int32)).astype(jnp.float32).astype(jnp.bfloat16)
        total = dot(valid_ref[...], rows, NT) + dot(y_ref[...], jnp.concatenate([t_hot] * 3, axis=0))
        at = pl.ds(pl.multiple_of(m * chunk, chunk), chunk)
        cost[:, at] = total * (2.0 * kap)
        norm_ref[:, at] = labels[1:2]

    def build(d):
        here = nc * n // chunk
        loop(0, here, lambda m: build_chunk(row_from(d) * here + m))
        row_part(0, pl.ds(pl.multiple_of(row_from(d) * here * chunk, chunk), here * chunk), here * chunk)

    def fold(op, values):
        while len(values) > 1:
            values = [op(*values[k:k + 2]) if k + 1 < len(values) else values[k]
                      for k in range(0, len(values), 2)]
        return values[0]

    def row_part(e, at, span):
        def term(k):
            rows = pl.ds(pl.multiple_of(k * 8, 8), 8)
            pot = b_ref[rows, :]
            return cost[rows, at] + jnp.concatenate([pot] * (span // LANES), axis=1)

        def sweep(op, start, value):
            step = math.gcd(nv // 8, 8)

            def body(k, state):
                return op(state, fold(op, [value(k * step + q) for q in range(step)]))

            return lax.fori_loop(0, nv // 8 // step, body, jnp.full((8, span), start, jnp.float32), unroll=2)

        high = jnp.max(sweep(jnp.maximum, -jnp.inf, term), axis=0, keepdims=True)
        wide_high = jnp.broadcast_to(high, (8, span))
        total = sweep(jnp.add, 0.0, lambda k: jnp.exp2(term(k) - wide_high))
        total = jnp.sum(total, axis=0, keepdims=True)
        pbuf[e, c, :, at] = high + log2(total)

    if square:
        from_row(1)
        from_row(2)
        relay(0)
        from_row(3)
        relay(1)
        complete(0)
        build(0)
        relay(2)
        complete(1)
        build(1)
        relay(3)
        complete(2)
        build(2)
        complete(3)
        build(3)
    else:
        loop(1, nr, from_row)
        loop(0, nr, relay)
        loop(0, nr, complete)
        loop(0, nr, build)
    a_ref[0] = -norm_ref[...]

    full_rows = nt
    full_cols = nv * nr * nc
    span = math.gcd(nt, 1024)

    def row_side(e):
        for w in range(nt // span):
            row_part(e, slice(w * span, (w + 1) * span), span)

    def lanes(x):
        return [x[:, k:k + LANES] for k in range(0, x.shape[1], LANES)]

    def col_side(a):
        pot = jnp.broadcast_to(a, (8, nt))

        def highest(k, _):
            rows = pl.ds(pl.multiple_of(k * 8, 8), 8)
            part_ref[rows, :] = fold(jnp.maximum, lanes(cost[rows, :] + pot))
            return 0

        lax.fori_loop(0, nv // 8, highest, 0, unroll=4)
        high_ref[...] = jnp.broadcast_to(jnp.max(part_ref[...], axis=1, keepdims=True), high_ref.shape)

        def summed(k, _):
            rows = pl.ds(pl.multiple_of(k * 8, 8), 8)
            high = high_ref[rows, :]
            part_ref[rows, :] = fold(jnp.add, [jnp.exp2(x - high) for x in lanes(cost[rows, :] + pot)])
            return 0

        lax.fori_loop(0, nv // 8, summed, 0, unroll=4)
        total = jnp.broadcast_to(jnp.sum(part_ref[...], axis=1, keepdims=True), part_ref.shape)
        b_ref[...] = 0.5 * (b_ref[...] + (math.log2(full_rows) - (high_ref[...] + log2(total))))

    def p_copy(e, d, to):
        src = c if to else (c + nc - d) % nc
        return rc(pbuf.at[e, src], pbuf.at[e, src], psend.at[e, d], precv.at[e, d], r, (c + d) % nc)

    def z_copy(e, d, to):
        src = r if to else (r + nr - d) % nr
        return rc(zbuf.at[e, src], zbuf.at[e, src], zsend.at[e, d], zrecv.at[e, d], (r + d) % nr, c)

    def joined(parts):
        high = jnp.max(parts, axis=0)
        return high + log2(jnp.sum(jnp.exp2(parts - high[None]), axis=0))

    def send_plane(e):
        loop(1, nc, lambda d: p_copy(e, d, True).start())

    def turn(e):
        loop(1, nc, lambda d: p_copy(e, d, False).wait_recv())
        zbuf[e, r] = joined(pbuf[e])
        loop(1, nr, lambda d: z_copy(e, d, True).start())

    def finish(e):
        loop(1, nr, lambda d: z_copy(e, d, False).wait_recv())
        a_ref[e + 1] = 0.5 * (a_ref[e] + (math.log2(full_cols) - joined(zbuf[e])))

    send_plane(0)
    col_side(a_ref[0])
    row_side(1)
    send_plane(1)
    for e in range(0, ITERS, 2):
        turn(e)
        turn(e + 1)
        finish(e)
        if e + 2 < ITERS:
            col_side(a_ref[e + 1])
            row_side(e + 2)
            send_plane(e + 2)
        finish(e + 1)
        if e + 3 < ITERS:
            col_side(a_ref[e + 2])
            row_side(e + 3)
            send_plane(e + 3)

    row_pot = (a_ref[ITERS] + norm_ref[...]) * (1.0 / SCALE)
    result = (row_pot * full_rows - jnp.sum(row_pot, axis=1, keepdims=True)) * (1.0 / (full_rows - 1))
    norm_ref[...] = result
    span_out = nt // nr
    out_ref[...] = norm_ref[:, pl.ds(pl.multiple_of(r * span_out, span_out), span_out)]

    loop(1, nr, sent)
    loop(0, nr, lambda d: loop(1, nh, lambda e: sent(nr + d * nh + e)))
    loop(0, nr, lambda d: loop(0, nh, lambda e: sent(nr + nr * nh + d * nh + e)))
    for e in range(ITERS):
        loop(1, nc, lambda d: p_copy(e, d, True).wait_send())
        loop(1, nr, lambda d: z_copy(e, d, True).wait_send())


def solution(mesh):
    nr, nc = mesh.shape["row"], mesh.shape["col"]

    def shards(train_embed, valid_embed, train_labels, valid_labels, pair_level, level_cost):
        n, width = train_embed.shape
        nv = valid_embed.shape[0]
        nt = nr * nc * n
        vmem = pl.BlockSpec(memory_space=pltpu.VMEM)
        dma = pltpu.SemaphoreType.DMA
        sends = nr + nr * nc
        out = pl.pallas_call(
            functools.partial(kernel, nr, nc, n),
            out_shape=pltpu.VMEM((1, nt // nr), jnp.float32),
            in_specs=[pl.BlockSpec(memory_space=pl.ANY)] * 6,
            out_specs=vmem,
            scratch_shapes=[
                pltpu.VMEM((nr * nc, n, width), jnp.bfloat16),
                pltpu.VMEM((nr * nc, 2, n), jnp.float32),
                pltpu.VMEM((1, n), jnp.int32),
                pltpu.SMEM(level_cost.shape, jnp.float32),
                pltpu.VMEM(pair_level.shape, jnp.int32),
                pltpu.VMEM((nv, width), jnp.bfloat16),
                pltpu.VMEM((1, nv), jnp.int32),
                pltpu.VMEM((nv, nt), jnp.float32),
                pltpu.VMEM((nv, 3 * LANES), jnp.bfloat16),
                pltpu.VMEM((nv, LANES), jnp.float32),
                pltpu.VMEM((ITERS + 1, 1, nt), jnp.float32),
                pltpu.VMEM((1, nt), jnp.float32),
                pltpu.VMEM((LANES, LANES), jnp.float32),
                pltpu.VMEM((nv, LANES), jnp.float32),
                pltpu.VMEM((nv, LANES), jnp.float32),
                pltpu.VMEM((ITERS, nc, 1, nt), jnp.float32),
                pltpu.VMEM((ITERS, nr, 1, nt), jnp.float32),
                dma((6,)), dma((sends,)), dma((sends,)), dma((nr * nc,)), dma((nr * nc,)),
                dma((ITERS, nc)), dma((ITERS, nc)), dma((ITERS, nr)), dma((ITERS, nr)),
            ],
            compiler_params=pltpu.CompilerParams(
                collective_id=0, has_side_effects=True, vmem_limit_bytes=56 * 1024 * 1024),
            name="sinkhorn",
        )(level_cost, pair_level, train_embed, train_labels[None, :], valid_embed, valid_labels[None, :])
        return out.reshape(nt // nr)

    placed = (
        P(("row", "col"), None),
        P(("row", "col"), None),
        P(("row", "col")),
        P(("row", "col")),
        P(),
        P(),
    )
    return jax.shard_map(shards, mesh=mesh, in_specs=placed, out_specs=P("row"), check_vma=False)
```
